32 devices in a mesh: seq: 8 (over z, y), head: 4 (over x, core).
Axes of the slice: x: 2, y: 2, z: 4, core: 2. Of those that a mesh axis runs over, the one named last changes fastest.
Arguments:
- queries: bfloat16 [1280, 2560], P('seq', 'head'), may hold values from -48 to 48
- keys: bfloat16 [1280, 2560], P('seq', 'head'), may hold values from -9.625 to 9.625
- values: bfloat16 [1280, 2560], P('seq', 'head'), may hold values from -6 to 6
- out_weight: bfloat16 [2560, 5120], P('head'), may hold values from -0.125 to 0.125
Outputs:
- mixed: bfloat16 [1280, 5120], P('seq', 'head')
The draws below stay inside these ranges and needn't reach their ends.
All inputs are finite; a program needn't handle non-finite values.
Results may differ from the reference program's by a relative error of at most 0.015.
Values may be sent and summed in bfloat16 or wider, within the bound.
No kernel may reach another device: no remote copies, remote signals or barrier semaphores. Data moves between devices by JAX's collectives and lax.ppermute only.
A program may use at most 192 MiB of HBM per device.

```python
import math
import jax
import jax.numpy as jnp
from jax import lax

D = 5120
HD = 128
HEADS = 20
TOK_DEV = 160
TOKENS = 1280
N_SEQ = 8


def draw_pair(key):
    base = jax.random.fold_in(key, 7101)
    key_query, key_key, key_order = jax.random.split(base, 3)
    width = HEADS * HD
    order = jax.random.permutation(key_order, TOKENS)
    query_field = 1.6 * jnp.clip(jax.random.normal(key_query, (TOKENS, width), jnp.float32), -6.0, 6.0)
    key_field = 1.6 * jnp.clip(jax.random.normal(key_key, (TOKENS, width), jnp.float32), -6.0, 6.0)
    query_field = query_field.at[order[48], 0].set(48.0).at[order[49], 1].set(-48.0)
    key_field = key_field.at[order[50], 0].set(9.625).at[order[51], 1].set(-9.625)
    return (query_field, key_field)


def draw_queries(key, part):
    return draw_pair(key)[0].astype(jnp.bfloat16)


def draw_keys(key, part):
    return draw_pair(key)[1].astype(jnp.bfloat16)


def block_levels(stream_key, shape, cuts, least, high):
    def one(position, blocks):
        draws = jax.random.uniform(jax.random.fold_in(jax.random.fold_in(stream_key, 6), position), (blocks,), jnp.float32, least / len(cuts), high / len(cuts))
        return jnp.repeat(jnp.exp(draws), shape[position] // blocks).reshape((-1,) + (1,) * (len(shape) - position - 1))

    level = one(*cuts[0])
    for cut in cuts[1:]:
        level = level * one(*cut)
    return level


def gaussian(stream_key, dims, scale, most, pieces=(), kind=jnp.bfloat16):
    values = scale * jax.random.normal(stream_key, dims, jnp.float32)
    if pieces:
        values = values * block_levels(stream_key, dims, pieces, -0.22, 0.18)
    return jnp.clip(values, -most, most).astype(kind)


def setup_inputs(seed: int = 0) -> dict:
    key_list = jax.random.split(jax.random.key(seed), 5)
    queries = draw_queries(jax.random.fold_in(key_list[4], 71), 0)
    keys = draw_keys(jax.random.fold_in(key_list[4], 71), 0)
    values = gaussian(key_list[2], (TOKENS, HEADS * HD), 1.0, 6.0, ((0, 8), (1, 4)))
    out_weight = gaussian(key_list[3], (HEADS * HD, D), (HEADS * HD) ** -0.5, 0.125, ((0, 4),))
    return {"queries": queries, "keys": keys, "values": values, "out_weight": out_weight}


def block_partial(query_all, key_block, value_block):
    scale = 1.0 / math.sqrt(HD)
    scores = jnp.einsum('thd,bhd->htb', query_all, key_block.astype(jnp.float32)) * scale
    block_max = lax.optimization_barrier(jnp.max(scores, axis=-1))
    expo = jnp.exp(scores - block_max[..., None])
    block_total = lax.optimization_barrier(jnp.sum(expo, axis=-1))
    weights = lax.optimization_barrier(expo.astype(jnp.bfloat16)).astype(jnp.float32)
    summed = jnp.einsum('htb,bhd->thd', weights, value_block.astype(jnp.float32))
    partial_value = summed / jnp.transpose(block_total)[..., None]
    partial_value = lax.optimization_barrier(partial_value.astype(jnp.bfloat16)).astype(jnp.float32)
    block_log = jnp.transpose(block_max + jnp.log(block_total))
    return (partial_value, block_log)

def reference(queries, keys, values, out_weight):
    width = HEADS * HD
    query_all = queries.astype(jnp.float32).reshape(TOKENS, HEADS, HD)
    key_blocks = keys.reshape(N_SEQ, TOK_DEV, HEADS, HD)
    value_blocks = values.reshape(N_SEQ, TOK_DEV, HEADS, HD)

    def absorb(state, blocks_in):
        key_block, value_block = blocks_in
        partial_value, block_log = block_partial(query_all, key_block, value_block)
        run_log, accum = state
        new_log = jnp.logaddexp(run_log, block_log)
        accum = accum * jnp.exp(run_log - new_log)[..., None] + partial_value * jnp.exp(block_log - new_log)[..., None]
        return ((new_log, accum), None)
    start_state = (jnp.full((TOKENS, HEADS), -1e+30, jnp.float32), jnp.zeros((TOKENS, HEADS, HD), jnp.float32))
    final_state, unused = lax.scan(absorb, start_state, (key_blocks, value_blocks))
    attended = final_state[1].astype(jnp.bfloat16).reshape(TOKENS, width)
    return jnp.dot(attended, out_weight, preferred_element_type=jnp.float32).astype(jnp.bfloat16)
```

```python
import functools
import math

import jax
import jax.numpy as jnp
from jax import lax
from jax.experimental import pallas as pl
from jax.experimental.pallas import tpu as pltpu
from jax.sharding import PartitionSpec as P


HD = 128
VM = pl.BlockSpec(memory_space=pltpu.VMEM)
GRANT = 8 * 2**20


def params():
    return pltpu.CompilerParams(vmem_limit_bytes=GRANT)


def flash_kernel(heads, blocks, first, last, *refs):
    q_ref = refs[0]
    k_refs = refs[1 : 1 + blocks]
    v_refs = refs[1 + blocks : 1 + 2 * blocks]
    rest = refs[1 + 2 * blocks :]
    rows = q_ref.shape[0]
    if not first:
        acc_in, top_in, total_in = rest[:3]
        rest = rest[3:]
    factor = math.log2(math.e) / math.sqrt(HD)
    for h in range(heads):
        cols = slice(h * HD, (h + 1) * HD)
        key = jnp.concatenate([ref[:, cols] for ref in k_refs], axis=0)
        value = jnp.concatenate([ref[:, cols] for ref in v_refs], axis=0)
        scores = factor * lax.dot_general(
            q_ref[:, cols], key, (((1,), (1,)), ((), ())), preferred_element_type=jnp.float32
        )
        top = jnp.max(scores, axis=1, keepdims=True)
        if not first:
            old_top = top_in[:, cols]
            wide_top = jnp.maximum(jnp.broadcast_to(top, (rows, HD)), old_top)
            top = wide_top[:, :1]
        else:
            wide_top = jnp.broadcast_to(top, (rows, HD))
        expo = jnp.exp2(scores - top)
        total = jnp.broadcast_to(jnp.sum(expo, axis=1, keepdims=True), (rows, HD))
        summed = jnp.dot(expo.astype(jnp.bfloat16), value, preferred_element_type=jnp.float32)
        if not first:
            shrink = jnp.exp2(old_top - wide_top)
            total = total + shrink * total_in[:, cols]
            summed = summed + shrink * acc_in[:, cols]
        if last:
            rest[0][:, cols] = (summed * jnp.exp2(-jnp.log2(total))).astype(jnp.bfloat16)
        else:
            rest[0][:, cols] = summed
            rest[1][:, cols] = wide_top
            rest[2][:, cols] = total


def flash(query, keys, values, state, last):
    rows, width = query.shape
    heads = width // HD
    blocks = len(keys)
    count = sum(k.shape[0] for k in keys)
    if last:
        out_shape = jax.ShapeDtypeStruct((rows, width), jnp.bfloat16)
        out_specs = VM
    else:
        out_shape = [jax.ShapeDtypeStruct((rows, width), jnp.float32)] * 3
        out_specs = [VM] * 3
    args = (query, *keys, *values, *state)
    return pl.pallas_call(
        functools.partial(flash_kernel, heads, blocks, not state, last),
        out_shape=out_shape,
        in_specs=[VM] * len(args),
        out_specs=out_specs,
        cost_estimate=pl.CostEstimate(
            flops=4 * rows * count * width,
            transcendentals=rows * count * heads,
            bytes_accessed=2 * rows * width * (1 + 2 * blocks) + 24 * rows * width,
        ),
        compiler_params=params(),
        name="flash",
    )(*args)


def weights_kernel(chips, columns, w_ref, mine_ref, other_ref, sems):
    place = lax.axis_index("head")
    copies = []
    for p in range(chips):
        target = lax.rem(place // 2 + p + 1, chips)
        for side, out in enumerate((mine_ref, other_ref)):
            core = place % 2 if side == 0 else 1 - place % 2
            start = pl.multiple_of((2 * target + core) * columns, HD)
            copy = pltpu.make_async_copy(
                w_ref.at[:, pl.ds(start, columns)],
                out.at[:, pl.ds(p * columns, columns)],
                sems.at[2 * p + side],
            )
            copy.start()
            copies.append(copy)
    for copy in copies:
        copy.wait()


def split_weights(weight, chips, columns):
    depth = weight.shape[0]
    half = jax.ShapeDtypeStruct((depth, chips * columns), weight.dtype)
    return pl.pallas_call(
        functools.partial(weights_kernel, chips, columns),
        out_shape=(half, half),
        in_specs=[pl.BlockSpec(memory_space=pl.ANY)],
        out_specs=(VM, VM),
        scratch_shapes=[pltpu.SemaphoreType.DMA((2 * chips,))],
        cost_estimate=pl.CostEstimate(
            flops=0, transcendentals=0, bytes_accessed=8 * depth * chips * columns
        ),
        compiler_params=pltpu.CompilerParams(vmem_limit_bytes=2 * GRANT),
        name="split_weights",
    )(weight)


def project_kernel(first, tile, a_ref, w_ref, *refs):
    out_ref = refs[-1]
    for start in range(0, out_ref.shape[1], tile):
        value = jnp.dot(
            a_ref[...],
            w_ref[:, first + start : first + start + tile],
            preferred_element_type=jnp.float32,
        )
        if len(refs) > 1:
            value = value + refs[0][:, start : start + tile]
        out_ref[:, start : start + tile] = value.astype(out_ref.dtype)


def project(rows_in, weight, first, columns, base, dtype):
    rows, depth = rows_in.shape
    tile = 256 if columns % 256 == 0 else HD
    args = (rows_in, weight) if base is None else (rows_in, weight, base)
    return pl.pallas_call(
        functools.partial(project_kernel, first, tile),
        out_shape=jax.ShapeDtypeStruct((rows, columns), dtype),
        in_specs=[VM] * len(args),
        out_specs=VM,
        cost_estimate=pl.CostEstimate(
            flops=2 * rows * depth * columns,
            transcendentals=0,
            bytes_accessed=2 * depth * columns + 4 * rows * columns,
        ),
        compiler_params=params(),
        name="project",
    )(*args)


def finish_kernel(arrived, *refs):
    total = refs[0][...]
    for ref in refs[1 : 1 + arrived]:
        total = total + ref[...].astype(jnp.float32)
    refs[-1][...] = total.astype(refs[-1].dtype)


def finish(mine, parts, index, pieces, output):
    rows, columns = mine.shape
    args = (mine, *parts)
    specs = [VM] * len(args)
    aliases = {}
    if output is not None:
        aliases = {len(args): 0}
        args += (output,)
        specs.append(pl.BlockSpec(memory_space=pl.ANY))
    return pl.pallas_call(
        functools.partial(finish_kernel, len(parts)),
        out_shape=jax.ShapeDtypeStruct((rows, columns * pieces), jnp.bfloat16),
        grid=(1,),
        in_specs=specs,
        out_specs=pl.BlockSpec((rows, columns), lambda i: (0, index)),
        input_output_aliases=aliases,
        cost_estimate=pl.CostEstimate(
            flops=rows * columns, transcendentals=0, bytes_accessed=8 * rows * columns
        ),
        compiler_params=params(),
        name="finish",
    )(*args)


def ring_pairs(n):
    order = list(range(0, n, 2)) + list(range(1, n, 2))[::-1]
    ahead = [(order[i], order[(i + 1) % n]) for i in range(n)]
    return ahead, [(b, a) for a, b in ahead]


def on_device(n_seq, n_head, queries, keys, values, out_weight):
    ahead, back = ring_pairs(n_seq)
    columns = out_weight.shape[1] // n_head
    chips = n_head // 2
    swap = [(i, i ^ 1) for i in range(n_head)]
    pieces = 2
    piece = columns // pieces
    steps = n_seq // 2

    w_mine, w_give = split_weights(out_weight, chips, columns)
    w_partner = lax.ppermute(w_give, "head", swap)
    state = flash(queries, [keys], [values], (), False)
    kf = kb = keys
    vf = vb = values
    for _ in range(1, steps):
        kf = lax.ppermute(kf, "seq", ahead)
        vb = lax.ppermute(vb, "seq", back)
        vf = lax.ppermute(vf, "seq", ahead)
        kb = lax.ppermute(kb, "seq", back)
        state = flash(queries, [kf, kb], [vf, vb], state, False)
    kf = lax.ppermute(kf, "seq", ahead)
    vb = lax.ppermute(vb, "seq", back)
    attended = flash(queries, [kf], [vb], state, True)
    partner = lax.ppermute(attended, "head", swap)

    arrived = [[] for _ in range(pieces)]
    for hop in range(1, chips):
        pairs = [(i, (i + 2 * hop) % n_head) for i in range(n_head)]
        for index in range(pieces):
            first = (hop - 1) * columns + index * piece
            part = project(attended, w_mine, first, piece, None, jnp.float32)
            part = project(partner, w_partner, first, piece, part, jnp.bfloat16)
            arrived[index].append(lax.ppermute(part, "head", pairs))
    output = None
    for index in range(pieces):
        first = (chips - 1) * columns + index * piece
        total = project(attended, w_mine, first, piece, None, jnp.float32)
        total = project(partner, w_partner, first, piece, total, jnp.float32)
        output = finish(total, arrived[index], index, pieces, output)
    return output


def solution(mesh):
    n_seq, n_head = mesh.shape["seq"], mesh.shape["head"]
    placed = (P("seq", "head"), P("seq", "head"), P("seq", "head"), P("head", None))
    return jax.shard_map(
        functools.partial(on_device, n_seq, n_head),
        mesh=mesh,
        in_specs=placed,
        out_specs=P("seq", "head"),
        check_vma=False,
    )
```

```python
import functools
import math

import jax
import jax.numpy as jnp
from jax import lax
from jax.experimental import pallas as pl
from jax.experimental.pallas import tpu as pltpu
from jax.sharding import PartitionSpec as P


HD = 128
VM = pl.BlockSpec(memory_space=pltpu.VMEM)
GRANT = 8 * 2**20
PIECE = 512


def params():
    return pltpu.CompilerParams(vmem_limit_bytes=GRANT)


def flash_kernel(heads, blocks, first, *refs):
    q_ref = refs[0]
    k_refs = refs[1 : 1 + blocks]
    v_refs = refs[1 + blocks : 1 + 2 * blocks]
    rest = refs[1 + 2 * blocks :]
    rows = q_ref.shape[0]
    if not first:
        acc_in, top_in, total_in = rest[:3]
        rest = rest[3:]
    acc_ref, top_ref, total_ref = rest
    for h in range(heads):
        cols = slice(h * HD, (h + 1) * HD)
        key = jnp.concatenate([ref[:, cols] for ref in k_refs], axis=0)
        value = jnp.concatenate([ref[:, cols] for ref in v_refs], axis=0)
        scores = score(q_ref[:, cols], key)
        top = jnp.broadcast_to(jnp.max(scores, axis=1, keepdims=True), (rows, HD))
        if not first:
            old_top = top_in[:, cols]
            top = jnp.maximum(top, old_top)
        expo = jnp.exp2(scores - top[:, :1])
        total = jnp.broadcast_to(jnp.sum(expo, axis=1, keepdims=True), (rows, HD))
        summed = jnp.dot(expo.astype(jnp.bfloat16), value, preferred_element_type=jnp.float32)
        if not first:
            shrink = jnp.exp2(old_top - top)
            total = total + shrink * total_in[:, cols]
            summed = summed + shrink * acc_in[:, cols]
        acc_ref[:, cols] = summed
        top_ref[:, cols] = top
        total_ref[:, cols] = total


def score(query, key):
    factor = math.log2(math.e) / math.sqrt(HD)
    return factor * lax.dot_general(
        query, key, (((1,), (1,)), ((), ())), preferred_element_type=jnp.float32
    )


def flash(query, keys, values, state):
    rows, width = query.shape
    heads = width // HD
    blocks = len(keys)
    count = sum(k.shape[0] for k in keys)
    args = (query, *keys, *values, *state)
    return pl.pallas_call(
        functools.partial(flash_kernel, heads, blocks, not state),
        out_shape=[jax.ShapeDtypeStruct((rows, width), jnp.float32)] * 3,
        in_specs=[VM] * len(args),
        out_specs=[VM] * 3,
        cost_estimate=pl.CostEstimate(
            flops=4 * rows * count * width,
            transcendentals=rows * count * heads,
            bytes_accessed=2 * rows * width * (1 + 2 * blocks) + 24 * rows * width,
        ),
        compiler_params=params(),
        name="flash",
    )(*args)


def last_scores_kernel(heads, q_ref, k_ref, acc_in, top_in, total_in, expo_ref, acc_ref, norm_ref):
    rows = q_ref.shape[0]
    for h in range(heads):
        cols = slice(h * HD, (h + 1) * HD)
        scores = score(q_ref[:, cols], k_ref[:, cols])
        old_top = top_in[:, cols]
        top = jnp.broadcast_to(jnp.max(scores, axis=1, keepdims=True), (rows, HD))
        top = jnp.maximum(top, old_top)
        expo = jnp.exp2(scores - top[:, :1])
        total = jnp.broadcast_to(jnp.sum(expo, axis=1, keepdims=True), (rows, HD))
        shrink = jnp.exp2(old_top - top)
        norm = jnp.exp2(-jnp.log2(total + shrink * total_in[:, cols]))
        expo_ref[h] = expo.astype(jnp.bfloat16)
        acc_ref[:, cols] = acc_in[:, cols] * (shrink * norm)
        norm_ref[:, cols] = norm


def last_scores(query, keys, state):
    rows, width = query.shape
    heads = width // HD
    count = keys.shape[0]
    wide = jax.ShapeDtypeStruct((rows, width), jnp.float32)
    return pl.pallas_call(
        functools.partial(last_scores_kernel, heads),
        out_shape=(jax.ShapeDtypeStruct((heads, rows, count), jnp.bfloat16), wide, wide),
        in_specs=[VM] * 5,
        out_specs=(VM,) * 3,
        cost_estimate=pl.CostEstimate(
            flops=2 * rows * count * width,
            transcendentals=rows * count * heads,
            bytes_accessed=24 * rows * width,
        ),
        compiler_params=params(),
        name="last_scores",
    )(query, keys, *state)


def last_values_kernel(heads, expo_ref, v_ref, acc_ref, norm_ref, out_ref):
    for h in range(heads):
        cols = slice(h * HD, (h + 1) * HD)
        summed = jnp.dot(expo_ref[h], v_ref[:, cols], preferred_element_type=jnp.float32)
        out_ref[:, cols] = (acc_ref[:, cols] + summed * norm_ref[:, cols]).astype(out_ref.dtype)


def last_values(expo, values, acc, norm):
    heads, rows, count = expo.shape
    width = heads * HD
    return pl.pallas_call(
        functools.partial(last_values_kernel, heads),
        out_shape=jax.ShapeDtypeStruct((rows, width), jnp.bfloat16),
        in_specs=[VM] * 4,
        out_specs=VM,
        cost_estimate=pl.CostEstimate(
            flops=2 * rows * count * width, transcendentals=0, bytes_accessed=14 * rows * width
        ),
        compiler_params=params(),
        name="last_values",
    )(expo, values, acc, norm)


def weights_kernel(chips, columns, w_ref, mine_ref, other_ref, sems):
    place = lax.axis_index("head")
    copies = []
    for p in range(chips):
        target = lax.rem(place // 2 + p + 1, chips)
        for side, out in enumerate((mine_ref, other_ref)):
            core = place % 2 if side == 0 else 1 - place % 2
            start = pl.multiple_of((2 * target + core) * columns, HD)
            copy = pltpu.make_async_copy(
                w_ref.at[:, pl.ds(start, columns)],
                out.at[:, pl.ds(p * columns, columns)],
                sems.at[2 * p + side],
            )
            copy.start()
            copies.append(copy)
    for copy in copies:
        copy.wait()


def split_weights(weight, chips, columns):
    depth = weight.shape[0]
    half = jax.ShapeDtypeStruct((depth, chips * columns), weight.dtype)
    return pl.pallas_call(
        functools.partial(weights_kernel, chips, columns),
        out_shape=(half, half),
        in_specs=[pl.BlockSpec(memory_space=pl.ANY)],
        out_specs=(VM, VM),
        scratch_shapes=[pltpu.SemaphoreType.DMA((2 * chips,))],
        cost_estimate=pl.CostEstimate(
            flops=0, transcendentals=0, bytes_accessed=8 * depth * chips * columns
        ),
        compiler_params=pltpu.CompilerParams(vmem_limit_bytes=2 * GRANT),
        name="split_weights",
    )(weight)


def project_kernel(first, tile, skip, a_ref, w_ref, *refs):
    out_ref = refs[-1]
    for start in range(0, out_ref.shape[1], tile):
        value = jnp.dot(
            a_ref[...],
            w_ref[:, first + start : first + start + tile],
            preferred_element_type=jnp.float32,
        )
        if len(refs) > 1:
            value = value + refs[0][:, skip + start : skip + start + tile]
        out_ref[:, start : start + tile] = value.astype(out_ref.dtype)


def project(rows_in, weight, first, columns, base, skip, dtype):
    rows, depth = rows_in.shape
    tile = 256 if columns % 256 == 0 else HD
    args = (rows_in, weight) if base is None else (rows_in, weight, base)
    return pl.pallas_call(
        functools.partial(project_kernel, first, tile, skip),
        out_shape=jax.ShapeDtypeStruct((rows, columns), dtype),
        in_specs=[VM] * len(args),
        out_specs=VM,
        cost_estimate=pl.CostEstimate(
            flops=2 * rows * depth * columns,
            transcendentals=0,
            bytes_accessed=2 * depth * columns + 4 * rows * columns,
        ),
        compiler_params=params(),
        name="project",
    )(*args)


def finish_kernel(skip, arrived, *refs):
    columns = refs[-1].shape[1]
    total = refs[0][:, skip : skip + columns]
    for ref in refs[1 : 1 + arrived]:
        total = total + ref[...].astype(jnp.float32)
    refs[-1][...] = total.astype(refs[-1].dtype)


def finish(mine, parts, start, columns, output):
    rows = mine.shape[0]
    args = (mine, *parts)
    specs = [VM] * len(args)
    aliases = {}
    if output is not None:
        aliases = {len(args): 0}
        args += (output,)
        specs.append(pl.BlockSpec(memory_space=pl.ANY))
    return pl.pallas_call(
        functools.partial(finish_kernel, start, len(parts)),
        out_shape=jax.ShapeDtypeStruct(mine.shape, jnp.bfloat16),
        grid=(1,),
        in_specs=specs,
        out_specs=pl.BlockSpec((rows, columns), lambda i: (0, start // columns)),
        input_output_aliases=aliases,
        cost_estimate=pl.CostEstimate(
            flops=rows * columns, transcendentals=0, bytes_accessed=8 * rows * columns
        ),
        compiler_params=params(),
        name="finish",
    )(*args)


def column_pieces(columns):
    narrow = columns % PIECE or PIECE
    return [(columns - narrow, narrow)] + [(c, PIECE) for c in range(0, columns - narrow, PIECE)]


def ring_pairs(n):
    order = list(range(0, n, 2)) + list(range(1, n, 2))[::-1]
    ahead = [(order[i], order[(i + 1) % n]) for i in range(n)]
    return ahead, [(b, a) for a, b in ahead]


def on_device(n_seq, n_head, queries, keys, values, out_weight):
    ahead, back = ring_pairs(n_seq)
    columns = out_weight.shape[1] // n_head
    chips = n_head // 2
    swap = [(i, i ^ 1) for i in range(n_head)]
    pieces = column_pieces(columns)
    steps = n_seq // 2

    w_mine, w_give = split_weights(out_weight, chips, columns)
    w_partner = lax.ppermute(w_give, "head", swap)
    state = flash(queries, [keys], [values], ())
    kf = kb = keys
    vf = vb = values
    for _ in range(1, steps):
        kf = lax.ppermute(kf, "seq", ahead)
        vb = lax.ppermute(vb, "seq", back)
        vf = lax.ppermute(vf, "seq", ahead)
        kb = lax.ppermute(kb, "seq", back)
        state = flash(queries, [kf, kb], [vf, vb], state)
    kf = lax.ppermute(kf, "seq", ahead)
    vb = lax.ppermute(vb, "seq", back)
    expo, acc, norm = last_scores(queries, kf, state)
    attended = last_values(expo, vb, acc, norm)
    partner = lax.ppermute(attended, "head", swap)

    away = (chips - 1) * columns
    part = project(attended, w_mine, 0, away, None, 0, jnp.float32)
    arrived = [[] for _ in pieces]
    for index, (start, piece) in enumerate(pieces):
        for hop in range(1, chips):
            pairs = [(i, (i + 2 * hop) % n_head) for i in range(n_head)]
            first = (hop - 1) * columns + start
            given = project(partner, w_partner, first, piece, part, first, jnp.bfloat16)
            arrived[index].append(lax.ppermute(given, "head", pairs))
    total = project(attended, w_mine, away, columns, None, 0, jnp.float32)
    total = project(partner, w_partner, away, columns, total, 0, jnp.float32)
    output = None
    for index, (start, piece) in enumerate(pieces):
        output = finish(total, arrived[index], start, piece, output)
    return output


def solution(mesh):
    n_seq, n_head = mesh.shape["seq"], mesh.shape["head"]
    placed = (P("seq", "head"), P("seq", "head"), P("seq", "head"), P("head", None))
    return jax.shard_map(
        functools.partial(on_device, n_seq, n_head),
        mesh=mesh,
        in_specs=placed,
        out_specs=P("seq", "head"),
        check_vma=False,
    )
```

```python
import functools
import math

import jax
import jax.numpy as jnp
from jax import lax
from jax.experimental import pallas as pl
from jax.experimental.pallas import tpu as pltpu
from jax.sharding import PartitionSpec as P


HD = 128
VM = pl.BlockSpec(memory_space=pltpu.VMEM)
HBM = pl.BlockSpec(memory_space=pltpu.HBM)
GRANT = 8 * 2**20
PIECE = 512


def params():
    return pltpu.CompilerParams(vmem_limit_bytes=GRANT)


def flash_kernel(heads, blocks, first, *refs):
    q_ref = refs[0]
    k_refs = refs[1 : 1 + blocks]
    v_refs = refs[1 + blocks : 1 + 2 * blocks]
    rest = refs[1 + 2 * blocks :]
    rows = q_ref.shape[0]
    if not first:
        acc_in, top_in, total_in = rest[:3]
        rest = rest[3:]
    acc_ref, top_ref, total_ref = rest

    def part(h):
        return slice(h * HD, (h + 1) * HD)

    def scores_of(h):
        key = jnp.concatenate([ref[:, part(h)] for ref in k_refs], axis=0)
        return score(q_ref[:, part(h)], key)

    def weights_of(h, scores):
        top = jnp.broadcast_to(jnp.max(scores, axis=1, keepdims=True), (rows, HD))
        shrink = None
        if not first:
            old_top = top_in[:, part(h)]
            top = jnp.maximum(top, old_top)
            shrink = jnp.exp2(old_top - top)
        expo = jnp.exp2(scores - spread(top, scores.shape[1]))
        total = jnp.broadcast_to(jnp.sum(expo, axis=1, keepdims=True), (rows, HD))
        if not first:
            total = total + shrink * total_in[:, part(h)]
        top_ref[:, part(h)] = top
        total_ref[:, part(h)] = total
        return expo.astype(jnp.bfloat16), shrink

    def values_of(h, expo, shrink):
        value = jnp.concatenate([ref[:, part(h)] for ref in v_refs], axis=0)
        summed = jnp.dot(expo, value, preferred_element_type=jnp.float32)
        if not first:
            summed = summed + shrink * acc_in[:, part(h)]
        acc_ref[:, part(h)] = summed

    ahead = scores_of(0)
    weights = None
    for h in range(heads):
        scores = ahead
        if h + 1 < heads:
            ahead = scores_of(h + 1)
        made = weights_of(h, scores)
        if weights is not None:
            values_of(h - 1, *weights)
        weights = made
    values_of(heads - 1, *weights)


def spread(value, count):
    whole, rest = divmod(count, HD)
    pieces = [value] * whole + ([value[:, :rest]] if rest else [])
    return jnp.concatenate(pieces, axis=1)


def score(query, key):
    factor = math.log2(math.e) / math.sqrt(HD)
    return factor * lax.dot_general(
        query, key, (((1,), (1,)), ((), ())), preferred_element_type=jnp.float32
    )


def flash(query, keys, values, state):
    rows, width = query.shape
    heads = width // HD
    blocks = len(keys)
    count = sum(k.shape[0] for k in keys)
    args = (query, *keys, *values, *state)
    return pl.pallas_call(
        functools.partial(flash_kernel, heads, blocks, not state),
        out_shape=[jax.ShapeDtypeStruct((rows, width), jnp.float32)] * 3,
        in_specs=[VM] * len(args),
        out_specs=[VM] * 3,
        cost_estimate=pl.CostEstimate(
            flops=4 * rows * count * width,
            transcendentals=rows * count * heads,
            bytes_accessed=2 * rows * width * (1 + 2 * blocks) + 24 * rows * width,
        ),
        compiler_params=params(),
        name="flash",
    )(*args)


def first_flash_kernel(heads, q_hbm, k_hbm, v_hbm, acc, top, total, q_ref, k_ref, v_ref, sems):
    pairs = ((q_hbm, q_ref), (k_hbm, k_ref), (v_hbm, v_ref))
    copies = [pltpu.make_async_copy(a, b, sems.at[i]) for i, (a, b) in enumerate(pairs)]
    for copy in copies:
        copy.start()
    for copy in copies:
        copy.wait()
    flash_kernel(heads, 1, True, q_ref, k_ref, v_ref, acc, top, total)


def first_flash(query, keys, values):
    rows, width = query.shape
    heads = width // HD
    wide = jax.ShapeDtypeStruct((rows, width), jnp.float32)
    count = keys.shape[0]
    *state, query = pl.pallas_call(
        functools.partial(first_flash_kernel, heads),
        out_shape=(wide, wide, wide, jax.ShapeDtypeStruct(query.shape, query.dtype)),
        in_specs=[HBM] * 3,
        out_specs=[VM] * 4,
        scratch_shapes=[
            pltpu.VMEM(keys.shape, keys.dtype),
            pltpu.VMEM(values.shape, values.dtype),
            pltpu.SemaphoreType.DMA((3,)),
        ],
        cost_estimate=pl.CostEstimate(
            flops=4 * rows * count * width,
            transcendentals=rows * count * heads,
            bytes_accessed=20 * rows * width,
        ),
        compiler_params=params(),
        name="first_flash",
    )(*(pltpu.with_memory_space_constraint(a, pltpu.HBM) for a in (query, keys, values)))
    return query, state


def last_scores_kernel(heads, q_ref, k_ref, acc_in, top_in, total_in, expo_ref, acc_ref, norm_ref):
    rows = q_ref.shape[0]

    def part(h):
        return slice(h * HD, (h + 1) * HD)

    ahead = score(q_ref[:, part(0)], k_ref[:, part(0)])
    for h in range(heads):
        scores = ahead
        if h + 1 < heads:
            ahead = score(q_ref[:, part(h + 1)], k_ref[:, part(h + 1)])
        old_top = top_in[:, part(h)]
        top = jnp.broadcast_to(jnp.max(scores, axis=1, keepdims=True), (rows, HD))
        top = jnp.maximum(top, old_top)
        expo = jnp.exp2(scores - spread(top, scores.shape[1]))
        total = jnp.broadcast_to(jnp.sum(expo, axis=1, keepdims=True), (rows, HD))
        shrink = jnp.exp2(old_top - top)
        norm = pl.reciprocal(total + shrink * total_in[:, part(h)])
        expo_ref[h] = expo.astype(jnp.bfloat16)
        acc_ref[:, part(h)] = acc_in[:, part(h)] * (shrink * norm)
        norm_ref[:, part(h)] = norm


def last_scores(query, keys, state):
    rows, width = query.shape
    heads = width // HD
    count = keys.shape[0]
    wide = jax.ShapeDtypeStruct((rows, width), jnp.float32)
    return pl.pallas_call(
        functools.partial(last_scores_kernel, heads),
        out_shape=(jax.ShapeDtypeStruct((heads, rows, count), jnp.bfloat16), wide, wide),
        in_specs=[VM] * 5,
        out_specs=(VM,) * 3,
        cost_estimate=pl.CostEstimate(
            flops=2 * rows * count * width,
            transcendentals=rows * count * heads,
            bytes_accessed=24 * rows * width,
        ),
        compiler_params=params(),
        name="last_scores",
    )(query, keys, *state)


def last_values_kernel(heads, expo_ref, upper_ref, lower_ref, acc_ref, norm_ref, out_ref):
    for h in range(heads):
        cols = slice(h * HD, (h + 1) * HD)
        value = jnp.concatenate([upper_ref[:, cols], lower_ref[:, cols]], axis=0)
        summed = jnp.dot(expo_ref[h], value, preferred_element_type=jnp.float32)
        out_ref[:, cols] = (acc_ref[:, cols] + summed * norm_ref[:, cols]).astype(out_ref.dtype)


def last_values(expo, upper, lower, acc, norm):
    heads, rows, count = expo.shape
    width = heads * HD
    return pl.pallas_call(
        functools.partial(last_values_kernel, heads),
        out_shape=jax.ShapeDtypeStruct((rows, width), jnp.bfloat16),
        in_specs=[VM] * 5,
        out_specs=VM,
        cost_estimate=pl.CostEstimate(
            flops=2 * rows * count * width, transcendentals=0, bytes_accessed=14 * rows * width
        ),
        compiler_params=params(),
        name="last_values",
    )(expo, upper, lower, acc, norm)


def columns_kernel(chips, columns, partner, w_ref, out_ref, sems):
    place = lax.axis_index("head")
    core = 1 - place % 2 if partner else place % 2
    copies = []
    for p in range(chips):
        target = lax.rem(place // 2 + p + 1, chips)
        start = pl.multiple_of((2 * target + core) * columns, HD)
        copies.append(
            pltpu.make_async_copy(
                w_ref.at[:, pl.ds(start, columns)],
                out_ref.at[:, pl.ds(p * columns, columns)],
                sems.at[p],
            )
        )
        copies[-1].start()
    for copy in copies:
        copy.wait()


def weight_columns(weight, chips, columns, partner):
    depth = weight.shape[0]
    return pl.pallas_call(
        functools.partial(columns_kernel, chips, columns, partner),
        out_shape=jax.ShapeDtypeStruct((depth, chips * columns), weight.dtype),
        in_specs=[HBM],
        out_specs=VM,
        scratch_shapes=[pltpu.SemaphoreType.DMA((chips,))],
        cost_estimate=pl.CostEstimate(
            flops=0, transcendentals=0, bytes_accessed=4 * depth * chips * columns
        ),
        compiler_params=params(),
        name="weight_columns",
    )(pltpu.with_memory_space_constraint(weight, pltpu.HBM))


def project_kernel(first, tile, skip, a_ref, w_ref, *refs):
    out_ref = refs[-1]
    for start in range(0, out_ref.shape[1], tile):
        value = jnp.dot(
            a_ref[...],
            w_ref[:, first + start : first + start + tile],
            preferred_element_type=jnp.float32,
        )
        if len(refs) > 1:
            value = value + refs[0][:, skip + start : skip + start + tile]
        out_ref[:, start : start + tile] = value.astype(out_ref.dtype)


def project(rows_in, weight, first, columns, base, skip, dtype):
    rows, depth = rows_in.shape
    tile = 256 if columns % 256 == 0 else HD
    args = (rows_in, weight) if base is None else (rows_in, weight, base)
    return pl.pallas_call(
        functools.partial(project_kernel, first, tile, skip),
        out_shape=jax.ShapeDtypeStruct((rows, columns), dtype),
        in_specs=[VM] * len(args),
        out_specs=VM,
        cost_estimate=pl.CostEstimate(
            flops=2 * rows * depth * columns,
            transcendentals=0,
            bytes_accessed=2 * depth * columns + 4 * rows * columns,
        ),
        compiler_params=params(),
        name="project",
    )(*args)


def finish_kernel(skip, arrived, *refs):
    columns = refs[-1].shape[1]
    total = refs[0][:, skip : skip + columns]
    for ref in refs[1 : 1 + arrived]:
        total = total + ref[...].astype(jnp.float32)
    refs[-1][...] = total.astype(refs[-1].dtype)


def finish(mine, parts, start, columns, output):
    rows = mine.shape[0]
    args = (mine, *parts)
    specs = [VM] * len(args)
    aliases = {}
    if output is not None:
        aliases = {len(args): 0}
        args += (output,)
        specs.append(pl.BlockSpec(memory_space=pl.ANY))
    return pl.pallas_call(
        functools.partial(finish_kernel, start, len(parts)),
        out_shape=jax.ShapeDtypeStruct(mine.shape, jnp.bfloat16),
        grid=(1,),
        in_specs=specs,
        out_specs=pl.BlockSpec((rows, columns), lambda i: (0, start // columns)),
        input_output_aliases=aliases,
        cost_estimate=pl.CostEstimate(
            flops=rows * columns, transcendentals=0, bytes_accessed=8 * rows * columns
        ),
        compiler_params=params(),
        name="finish",
    )(*args)


def column_pieces(columns):
    narrow = columns % PIECE or PIECE
    return [(columns - narrow, narrow)] + [(c, PIECE) for c in range(0, columns - narrow, PIECE)]


def ring_pairs(n):
    order = list(range(0, n, 2)) + list(range(1, n, 2))[::-1]
    ahead = [(order[i], order[(i + 1) % n]) for i in range(n)]
    return ahead, [(b, a) for a, b in ahead]


def on_device(n_seq, n_head, queries, keys, values, out_weight):
    rows = queries.shape[0]
    ahead, back = ring_pairs(n_seq)
    columns = out_weight.shape[1] // n_head
    chips = n_head // 2
    swap = [(i, i ^ 1) for i in range(n_head)]
    pieces = column_pieces(columns)
    steps = n_seq // 2

    w_give = weight_columns(out_weight, chips, columns, True)
    w_mine = weight_columns(out_weight, chips, columns, False)
    w_partner = lax.ppermute(w_give, "head", swap)
    queries, state = first_flash(queries, keys, values)
    kf = kb = keys
    vf = vb = values
    for _ in range(1, steps):
        kf = lax.ppermute(kf, "seq", ahead)
        vb = lax.ppermute(vb, "seq", back)
        vf = lax.ppermute(vf, "seq", ahead)
        kb = lax.ppermute(kb, "seq", back)
        state = flash(queries, [kf, kb], [vf, vb], state)
    kf = lax.ppermute(kf, "seq", ahead)
    upper = rows * 4 // 5 // 16 * 16
    v_upper = lax.ppermute(vb[:upper], "seq", back)
    v_lower = lax.ppermute(vf[upper:], "seq", ahead)
    expo, acc, norm = last_scores(queries, kf, state)
    attended = last_values(expo, v_upper, v_lower, acc, norm)
    partner = lax.ppermute(attended, "head", swap)

    away = (chips - 1) * columns
    part = project(attended, w_mine, 0, away, None, 0, jnp.float32)
    arrived = [[] for _ in pieces]
    for index, (start, piece) in enumerate(pieces):
        for hop in range(1, chips):
            pairs = [(i, (i + 2 * hop) % n_head) for i in range(n_head)]
            first = (hop - 1) * columns + start
            given = project(partner, w_partner, first, piece, part, first, jnp.bfloat16)
            arrived[index].append(lax.ppermute(given, "head", pairs))
    total = project(attended, w_mine, away, columns, None, 0, jnp.float32)
    total = project(partner, w_partner, away, columns, total, 0, jnp.float32)
    output = None
    for index, (start, piece) in enumerate(pieces):
        output = finish(total, arrived[index], start, piece, output)
    return output


def solution(mesh):
    n_seq, n_head = mesh.shape["seq"], mesh.shape["head"]
    placed = (P("seq", "head"), P("seq", "head"), P("seq", "head"), P("head", None))
    return jax.shard_map(
        functools.partial(on_device, n_seq, n_head),
        mesh=mesh,
        in_specs=placed,
        out_specs=P("seq", "head"),
        check_vma=False,
    )
```

```python
import functools
import math

import jax
import jax.numpy as jnp
from jax import lax
from jax.experimental import pallas as pl
from jax.experimental.pallas import tpu as pltpu
from jax.sharding import PartitionSpec as P


HD = 128
VM = pl.BlockSpec(memory_space=pltpu.VMEM)
HBM = pl.BlockSpec(memory_space=pltpu.HBM)
GRANT = 8 * 2**20
PIECE = 512


def params():
    return pltpu.CompilerParams(vmem_limit_bytes=GRANT)


def flash_kernel(heads, blocks, first, *refs):
    q_ref = refs[0]
    k_refs = refs[1 : 1 + blocks]
    v_refs = refs[1 + blocks : 1 + 2 * blocks]
    rest = refs[1 + 2 * blocks :]
    rows = q_ref.shape[0]
    if not first:
        acc_in, top_in, total_in = rest[:3]
        rest = rest[3:]
    acc_ref, top_ref, total_ref = rest

    def part(h):
        return slice(h * HD, (h + 1) * HD)

    def scores_of(h):
        key = jnp.concatenate([ref[:, part(h)] for ref in k_refs], axis=0)
        return score(q_ref[:, part(h)], key)

    def weights_of(h, scores):
        top = jnp.broadcast_to(jnp.max(scores, axis=1, keepdims=True), (rows, HD))
        shrink = None
        if not first:
            old_top = top_in[:, part(h)]
            top = jnp.maximum(top, old_top)
            shrink = jnp.exp2(old_top - top)
        expo = jnp.exp2(scores - spread(top, scores.shape[1]))
        total = jnp.broadcast_to(jnp.sum(expo, axis=1, keepdims=True), (rows, HD))
        if not first:
            total = total + shrink * total_in[:, part(h)]
        top_ref[:, part(h)] = top
        total_ref[:, part(h)] = total
        return expo.astype(jnp.bfloat16), shrink

    def values_of(h, expo, shrink):
        value = jnp.concatenate([ref[:, part(h)] for ref in v_refs], axis=0)
        summed = jnp.dot(expo, value, preferred_element_type=jnp.float32)
        if not first:
            summed = summed + shrink * acc_in[:, part(h)]
        acc_ref[:, part(h)] = summed

    ahead = scores_of(0)
    weights = None
    for h in range(heads):
        scores = ahead
        if h + 1 < heads:
            ahead = scores_of(h + 1)
        made = weights_of(h, scores)
        if weights is not None:
            values_of(h - 1, *weights)
        weights = made
    values_of(heads - 1, *weights)


def spread(value, count):
    whole, rest = divmod(count, HD)
    pieces = [value] * whole + ([value[:, :rest]] if rest else [])
    return jnp.concatenate(pieces, axis=1)


def score(query, key):
    factor = math.log2(math.e) / math.sqrt(HD)
    return factor * lax.dot_general(
        query, key, (((1,), (1,)), ((), ())), preferred_element_type=jnp.float32
    )


def flash(query, keys, values, state):
    rows, width = query.shape
    heads = width // HD
    blocks = len(keys)
    count = sum(k.shape[0] for k in keys)
    args = (query, *keys, *values, *state)
    return pl.pallas_call(
        functools.partial(flash_kernel, heads, blocks, not state),
        out_shape=[jax.ShapeDtypeStruct((rows, width), jnp.float32)] * 3,
        in_specs=[VM] * len(args),
        out_specs=[VM] * 3,
        cost_estimate=pl.CostEstimate(
            flops=4 * rows * count * width,
            transcendentals=rows * count * heads,
            bytes_accessed=2 * rows * width * (1 + 2 * blocks) + 24 * rows * width,
        ),
        compiler_params=params(),
        name="flash",
    )(*args)


def first_flash_kernel(heads, q_hbm, k_hbm, v_hbm, acc, top, total, q_ref, k_ref, v_ref, sems):
    pairs = ((q_hbm, q_ref), (k_hbm, k_ref), (v_hbm, v_ref))
    copies = [pltpu.make_async_copy(a, b, sems.at[i]) for i, (a, b) in enumerate(pairs)]
    for copy in copies:
        copy.start()
    for copy in copies:
        copy.wait()
    flash_kernel(heads, 1, True, q_ref, k_ref, v_ref, acc, top, total)


def first_flash(query, keys, values):
    rows, width = query.shape
    heads = width // HD
    wide = jax.ShapeDtypeStruct((rows, width), jnp.float32)
    count = keys.shape[0]
    *state, query = pl.pallas_call(
        functools.partial(first_flash_kernel, heads),
        out_shape=(wide, wide, wide, jax.ShapeDtypeStruct(query.shape, query.dtype)),
        in_specs=[HBM] * 3,
        out_specs=[VM] * 4,
        scratch_shapes=[
            pltpu.VMEM(keys.shape, keys.dtype),
            pltpu.VMEM(values.shape, values.dtype),
            pltpu.SemaphoreType.DMA((3,)),
        ],
        cost_estimate=pl.CostEstimate(
            flops=4 * rows * count * width,
            transcendentals=rows * count * heads,
            bytes_accessed=20 * rows * width,
        ),
        compiler_params=params(),
        name="first_flash",
    )(*(pltpu.with_memory_space_constraint(a, pltpu.HBM) for a in (query, keys, values)))
    return query, state


def last_scores_kernel(heads, q_ref, k_ref, acc_in, top_in, total_in, expo_ref, acc_ref, norm_ref):
    rows = q_ref.shape[0]

    def part(h):
        return slice(h * HD, (h + 1) * HD)

    ahead = score(q_ref[:, part(0)], k_ref[:, part(0)])
    for h in range(heads):
        scores = ahead
        if h + 1 < heads:
            ahead = score(q_ref[:, part(h + 1)], k_ref[:, part(h + 1)])
        old_top = top_in[:, part(h)]
        top = jnp.broadcast_to(jnp.max(scores, axis=1, keepdims=True), (rows, HD))
        top = jnp.maximum(top, old_top)
        expo = jnp.exp2(scores - spread(top, scores.shape[1]))
        total = jnp.broadcast_to(jnp.sum(expo, axis=1, keepdims=True), (rows, HD))
        shrink = jnp.exp2(old_top - top)
        norm = pl.reciprocal(total + shrink * total_in[:, part(h)])
        expo_ref[h] = expo.astype(jnp.bfloat16)
        acc_ref[:, part(h)] = acc_in[:, part(h)] * (shrink * norm)
        norm_ref[:, part(h)] = norm


def last_scores(query, keys, state):
    rows, width = query.shape
    heads = width // HD
    count = keys.shape[0]
    wide = jax.ShapeDtypeStruct((rows, width), jnp.float32)
    return pl.pallas_call(
        functools.partial(last_scores_kernel, heads),
        out_shape=(jax.ShapeDtypeStruct((heads, rows, count), jnp.bfloat16), wide, wide),
        in_specs=[VM] * 5,
        out_specs=(VM,) * 3,
        cost_estimate=pl.CostEstimate(
            flops=2 * rows * count * width,
            transcendentals=rows * count * heads,
            bytes_accessed=24 * rows * width,
        ),
        compiler_params=pltpu.CompilerParams(vmem_limit_bytes=GRANT),
        name="last_scores",
    )(query, keys, *state)


def last_values_kernel(heads, expo_ref, upper_ref, lower_ref, acc_ref, norm_ref, out_ref):
    for h in range(heads):
        cols = slice(h * HD, (h + 1) * HD)
        value = jnp.concatenate([upper_ref[:, cols], lower_ref[:, cols]], axis=0)
        summed = jnp.dot(expo_ref[h], value, preferred_element_type=jnp.float32)
        out_ref[:, cols] = (acc_ref[:, cols] + summed * norm_ref[:, cols]).astype(out_ref.dtype)


def last_values(expo, upper, lower, acc, norm):
    heads, rows, count = expo.shape
    width = heads * HD
    return pl.pallas_call(
        functools.partial(last_values_kernel, heads),
        out_shape=jax.ShapeDtypeStruct((rows, width), jnp.bfloat16),
        in_specs=[VM] * 5,
        out_specs=VM,
        cost_estimate=pl.CostEstimate(
            flops=2 * rows * count * width, transcendentals=0, bytes_accessed=14 * rows * width
        ),
        compiler_params=params(),
        name="last_values",
    )(expo, upper, lower, acc, norm)


def columns_kernel(chips, columns, partner, w_ref, out_ref, sems):
    place = lax.axis_index("head")
    core = 1 - place % 2 if partner else place % 2
    copies = []
    for p in range(chips):
        target = lax.rem(place // 2 + p + 1, chips)
        start = pl.multiple_of((2 * target + core) * columns, HD)
        copies.append(
            pltpu.make_async_copy(
                w_ref.at[:, pl.ds(start, columns)],
                out_ref.at[:, pl.ds(p * columns, columns)],
                sems.at[p],
            )
        )
        copies[-1].start()
    for copy in copies:
        copy.wait()


def weight_columns(weight, chips, columns, partner):
    depth = weight.shape[0]
    return pl.pallas_call(
        functools.partial(columns_kernel, chips, columns, partner),
        out_shape=jax.ShapeDtypeStruct((depth, chips * columns), weight.dtype),
        in_specs=[HBM],
        out_specs=VM,
        scratch_shapes=[pltpu.SemaphoreType.DMA((chips,))],
        cost_estimate=pl.CostEstimate(
            flops=0, transcendentals=0, bytes_accessed=4 * depth * chips * columns
        ),
        compiler_params=params(),
        name="weight_columns",
    )(pltpu.with_memory_space_constraint(weight, pltpu.HBM))


def far_kernel(chips, columns, w_ref, *refs):
    place = lax.axis_index("head")
    outs, sems = refs[:-1], refs[-1]
    copies = []
    for i, out in enumerate(outs):
        target = lax.rem(place // 2 + i // 2 + 1, chips)
        core = place % 2 if i % 2 == 0 else 1 - place % 2
        start = pl.multiple_of((2 * target + core) * columns, HD)
        copies.append(
            pltpu.make_async_copy(w_ref.at[:, pl.ds(start, out.shape[1])], out, sems.at[i])
        )
        copies[-1].start()
    for copy in copies:
        copy.wait()


def far_columns(weight, chips, columns, far):
    depth = weight.shape[0]
    many = 2 * (chips - 1)
    return pl.pallas_call(
        functools.partial(far_kernel, chips, columns),
        out_shape=[jax.ShapeDtypeStruct((depth, far), weight.dtype)] * many,
        in_specs=[HBM],
        out_specs=[VM] * many,
        scratch_shapes=[pltpu.SemaphoreType.DMA((many,))],
        cost_estimate=pl.CostEstimate(
            flops=0, transcendentals=0, bytes_accessed=4 * depth * far * many
        ),
        compiler_params=params(),
        name="far_columns",
    )(pltpu.with_memory_space_constraint(weight, pltpu.HBM))


def project_kernel(first, tile, skip, a_ref, w_ref, *refs):
    out_ref = refs[-1]
    for start in range(0, out_ref.shape[1], tile):
        value = jnp.dot(
            a_ref[...],
            w_ref[:, first + start : first + start + tile],
            preferred_element_type=jnp.float32,
        )
        if len(refs) > 1:
            value = value + refs[0][:, skip + start : skip + start + tile]
        out_ref[:, start : start + tile] = value.astype(out_ref.dtype)


def project(rows_in, weight, first, columns, base, skip, dtype):
    rows, depth = rows_in.shape
    tile = 256 if columns % 256 == 0 else HD
    args = (rows_in, weight) if base is None else (rows_in, weight, base)
    return pl.pallas_call(
        functools.partial(project_kernel, first, tile, skip),
        out_shape=jax.ShapeDtypeStruct((rows, columns), dtype),
        in_specs=[VM] * len(args),
        out_specs=VM,
        cost_estimate=pl.CostEstimate(
            flops=2 * rows * depth * columns,
            transcendentals=0,
            bytes_accessed=2 * depth * columns + 4 * rows * columns,
        ),
        compiler_params=params(),
        name="project",
    )(*args)


def finish_kernel(skip, arrived, *refs):
    columns = refs[-1].shape[1]
    total = refs[0][:, skip : skip + columns]
    for ref in refs[1 : 1 + arrived]:
        total = total + ref[...].astype(jnp.float32)
    refs[-1][...] = total.astype(refs[-1].dtype)


def finish(mine, parts, start, columns, width, output):
    rows = mine.shape[0]
    args = (mine, *parts)
    specs = [VM] * len(args)
    aliases = {}
    if output is not None:
        aliases = {len(args): 0}
        args += (output,)
        specs.append(pl.BlockSpec(memory_space=pl.ANY))
    return pl.pallas_call(
        functools.partial(finish_kernel, start, len(parts)),
        out_shape=jax.ShapeDtypeStruct((rows, width), jnp.bfloat16),
        grid=(1,),
        in_specs=specs,
        out_specs=pl.BlockSpec((rows, columns), lambda i: (0, start // columns)),
        input_output_aliases=aliases,
        cost_estimate=pl.CostEstimate(
            flops=rows * columns, transcendentals=0, bytes_accessed=8 * rows * columns
        ),
        compiler_params=params(),
        name="finish",
    )(*args)


def far_width(columns):
    return columns * 2 // 5 // HD * HD


def column_pieces(columns):
    far = far_width(columns)
    narrow = (columns - far) % PIECE or PIECE
    return [(c, PIECE) for c in range(far, columns - narrow, PIECE)] + [(columns - narrow, narrow)]


def ring_pairs(n):
    order = list(range(0, n, 2)) + list(range(1, n, 2))[::-1]
    ahead = [(order[i], order[(i + 1) % n]) for i in range(n)]
    return ahead, [(b, a) for a, b in ahead]


def on_device(n_seq, n_head, queries, keys, values, out_weight):
    rows = queries.shape[0]
    ahead, back = ring_pairs(n_seq)
    columns = out_weight.shape[1] // n_head
    chips = n_head // 2
    swap = [(i, i ^ 1) for i in range(n_head)]
    pieces = column_pieces(columns)
    steps = n_seq // 2

    hops = range(1, chips)
    far = far_width(columns)
    far_pairs = [[(i, (i + 2 * hop) % n_head) for i in range(n_head)] for hop in hops]
    w_far = far_columns(out_weight, chips, columns, far)
    w_same = [lax.ppermute(w_far[2 * h - 2], "head", far_pairs[h - 1]) for h in hops]
    w_cross = [
        lax.ppermute(w_far[2 * h - 1], "head", [(a, b ^ 1) for a, b in far_pairs[h - 1]])
        for h in hops
    ]
    w_give = weight_columns(out_weight, chips, columns, True)
    w_mine = weight_columns(out_weight, chips, columns, False)
    w_partner = lax.ppermute(w_give, "head", swap)
    queries, state = first_flash(queries, keys, values)
    kf = kb = keys
    vf = vb = values
    for _ in range(1, steps):
        kf = lax.ppermute(kf, "seq", ahead)
        vb = lax.ppermute(vb, "seq", back)
        vf = lax.ppermute(vf, "seq", ahead)
        kb = lax.ppermute(kb, "seq", back)
        state = flash(queries, [kf, kb], [vf, vb], state)
    kf = lax.ppermute(kf, "seq", ahead)
    upper = rows * 4 // 5 // 16 * 16
    v_upper = lax.ppermute(vb[:upper], "seq", back)
    v_lower = lax.ppermute(vf[upper:], "seq", ahead)
    expo, acc, norm = last_scores(queries, kf, state)
    attended = last_values(expo, v_upper, v_lower, acc, norm)
    a_same = [lax.ppermute(attended, "head", far_pairs[h - 1]) for h in hops]
    partner = lax.ppermute(attended, "head", swap)

    away = (chips - 1) * columns
    part = project(attended, w_mine, 0, away, None, 0, jnp.float32)
    arrived = [[] for _ in pieces]
    for index, (start, piece) in enumerate(pieces):
        for hop in range(1, chips):
            pairs = [(i, (i + 2 * hop) % n_head) for i in range(n_head)]
            first = (hop - 1) * columns + start
            given = project(partner, w_partner, first, piece, part, first, jnp.bfloat16)
            arrived[index].append(lax.ppermute(given, "head", pairs))
    total = project(attended, w_mine, away, columns, None, 0, jnp.float32)
    total = project(partner, w_partner, away, columns, total, 0, jnp.float32)
    a_cross = [lax.ppermute(a_same[h - 1], "head", swap) for h in hops]
    near = total
    for h in hops:
        for far_rows, weight in ((a_same, w_same), (a_cross, w_cross)):
            near = project(far_rows[h - 1], weight[h - 1], 0, far, near, 0, jnp.float32)
    output = finish(near, [], 0, far, columns, None)
    for index, (start, piece) in enumerate(pieces):
        output = finish(total, arrived[index], start, piece, columns, output)
    return output


def solution(mesh):
    n_seq, n_head = mesh.shape["seq"], mesh.shape["head"]
    placed = (P("seq", "head"), P("seq", "head"), P("seq", "head"), P("head", None))
    return jax.shard_map(
        functools.partial(on_device, n_seq, n_head),
        mesh=mesh,
        in_specs=placed,
        out_specs=P("seq", "head"),
        check_vma=False,
    )
```
